32 devices in a mesh: heads: 4 (over x, core), seq: 8 (over z, y).
Axes of the slice: x: 2, y: 2, z: 4, core: 2. Of those that a mesh axis runs over, the one named last changes fastest.
Arguments:
- tokens: bfloat16 [2048, 4096], P('seq'), may hold values from -6 to 6
- norm_gain: float32 [4096], replicated, may hold values from 0.1 to 1.9
- w_query: bfloat16 [4096, 4096], P(None, 'heads'), may hold values from -0.09375 to 0.09375
- w_key: bfloat16 [4096, 1024], P(None, 'heads'), may hold values from -0.1875 to 0.1875
- w_value: bfloat16 [4096, 1024], P(None, 'heads'), may hold values from -0.375 to 0.375
- w_out: bfloat16 [4096, 4096], P('heads'), may hold values from -0.09375 to 0.09375
- cache_keys: bfloat16 [8, 8192, 128], P('heads', 'seq'), may hold values from -360 to 360
- cache_values: bfloat16 [8, 8192, 128], P('heads', 'seq'), may hold values from -24 to 24
- vert_blocks: int32 [8, 64], P('heads'), may hold values from -1 to 127, as said below
- vert_count: int32 [8], P('heads'), may hold values from 32 to 64
- slash_offsets: int32 [8, 4], P('heads'), may hold values from -1 to 4, as said below
- slash_count: int32 [8], P('heads'), may hold values from 1 to 4
Outputs:
- layer_out: bfloat16 [2048, 4096], P('seq', 'heads')
The draws below stay inside these ranges and needn't reach their ends.
Inputs may be any that keep to these rules, and one draw needn't show every extreme that they name: `vert_blocks`: row g lists cache blocks for key/value head g: its entries before vert_count[g] are distinct, the rest are -1. The cache of one index of seq holds at most 8 of the blocks that a row lists, and exactly 8 for one index in every row. `slash_offsets`: entries of row g before slash_count[g] are distinct, the rest are -1.
All inputs are finite; a program needn't handle non-finite values.
Results may differ from the reference program's by a relative error of at most 0.015.
The reference program's roundings to bfloat16 on the way count: a program that leaves them out, or rounds other values in their place, can miss the bound.
Values may be sent and summed in bfloat16 or wider, within the bound.
A program may use at most 64 MiB of HBM per device.

```python
import math
import jax
import jax.numpy as jnp
from jax import lax

D = 4096
QH = 32
KVH = 8
HD = 128
BLK = 64
NV = 64
VCAP = 8
SMAX = 4
CACHE_DEV = 1024
TOKENS = 2048
CACHE = 8192


def vertical_lists(key):
    base_key = jax.random.fold_in(key, 7)
    count_key, pick_key, hot_key, order_key, tie_key, mix_key = jax.random.split(base_key, 6)
    device_total = CACHE // CACHE_DEV
    per_device = CACHE_DEV // BLK
    counts = jax.random.randint(count_key, (KVH,), NV // 2, NV + 1)
    chosen_heads = jax.random.permutation(pick_key, KVH)
    counts = counts.at[chosen_heads[0]].set(NV).at[chosen_heads[1]].set(NV // 2)
    hot_device = jax.random.randint(hot_key, (KVH,), 0, device_total)
    order_scores = jax.random.randint(order_key, (KVH, device_total, per_device), 0, 2 ** 16) * per_device + jnp.arange(per_device)
    block_order = jnp.argsort(order_scores, axis=-1, stable=True)[:, :, :VCAP]
    candidate = jnp.arange(device_total)[None, :, None] * per_device + block_order
    hot_device_mask = jnp.arange(device_total)[None, :] == hot_device[:, None]
    priority = jnp.where(hot_device_mask[:, :, None], 0, 1 + jnp.arange(VCAP)[None, None, :])
    tie_break = jax.random.randint(tie_key, (KVH, device_total, VCAP), 0, 1024)
    flat_index = jnp.arange(device_total * VCAP).reshape(device_total, VCAP)[None]
    ranking = (priority * 1024 + tie_break) * (device_total * VCAP) + flat_index
    pick_order = jnp.argsort(ranking.reshape(KVH, -1), axis=-1, stable=True)[:, :NV]
    picked = jnp.take_along_axis(candidate.reshape(KVH, -1), pick_order, axis=1)
    positions = jnp.arange(NV)[None, :]
    live_entry = positions < counts[:, None]
    mixing = jnp.where(live_entry, jax.random.randint(mix_key, (KVH, NV), 0, 2 ** 12) * NV + positions, 2 ** 22 + positions)
    shuffle = jnp.argsort(mixing, axis=-1, stable=True)
    block_lists = jnp.take_along_axis(picked, shuffle, axis=1)
    return (jnp.where(live_entry, block_lists, -1).astype(jnp.int32), counts.astype(jnp.int32))


def slash_lists(key):
    base_key = jax.random.fold_in(key, 11)
    count_key, pick_key, order_key = jax.random.split(base_key, 3)
    counts = jax.random.randint(count_key, (KVH,), 1, SMAX + 1)
    chosen_heads = jax.random.permutation(pick_key, KVH)
    counts = counts.at[chosen_heads[0]].set(SMAX).at[chosen_heads[1]].set(1)
    scores = jax.random.randint(order_key, (KVH, SMAX), 0, 2 ** 16) * SMAX + jnp.arange(SMAX)
    offsets = jnp.argsort(scores, axis=-1, stable=True) + 1
    live_entry = jnp.arange(SMAX)[None, :] < counts[:, None]
    return (jnp.where(live_entry, offsets, -1).astype(jnp.int32), counts.astype(jnp.int32))


def draw_vert_blocks(key, part):
    return vertical_lists(key)[0]


def draw_vert_count(key, part):
    return vertical_lists(key)[1]


def draw_slash_offsets(key, part):
    return slash_lists(key)[0]


def draw_slash_count(key, part):
    return slash_lists(key)[1]


def draw_cache_keys(key, part):
    noise_key = jax.random.fold_in(jax.random.fold_in(key, 3), 0)
    values = jnp.clip(jax.random.normal(noise_key, (KVH, CACHE, HD), jnp.float32), -6.0, 6.0) * 2.0
    return values.astype(jnp.bfloat16)


def block_levels(own_key, shape, pieces, least, largest):
    level = 1.0
    for dim, shards_of in pieces:
        draws = jax.random.uniform(jax.random.fold_in(jax.random.fold_in(own_key, 6), dim), (shards_of,), jnp.float32, least / len(pieces), largest / len(pieces))
        level = level * jnp.repeat(jnp.exp(draws), shape[dim] // shards_of).reshape((-1,) + (1,) * (len(shape) - 1 - dim))
    return level


def noise(rng, shape, deviation, limit, pieces=(), held_as=jnp.bfloat16):
    drawn = jax.random.normal(rng, shape, jnp.float32) * deviation
    if len(pieces) > 0:
        drawn = block_levels(rng, shape, pieces, -0.22, 0.18) * drawn
    return jnp.clip(drawn, min=-limit, max=limit).astype(held_as)


def setup_inputs(seed: int = 0) -> dict:
    key_list = jax.random.split(jax.random.key(seed), 13)
    return {
        "tokens": noise(key_list[0], (TOKENS, D), 1.0, 6.0, ((0, 8),)),
        "norm_gain": jnp.clip(1.0 + 0.18 * jax.random.normal(key_list[1], (D,), jnp.float32), 0.1, 1.9),
        "w_query": noise(key_list[2], (D, QH * HD), D ** -0.5, 0.09375, ((1, 4),)),
        "w_key": noise(key_list[3], (D, KVH * HD), (D // 4) ** -0.5, 0.1875, ((1, 4),)),
        "w_value": noise(key_list[4], (D, KVH * HD), (D // 16) ** -0.5, 0.375, ((1, 4),)),
        "w_out": noise(key_list[5], (QH * HD, D), (QH * HD) ** -0.5, 0.09375, ((0, 4),)),
        "cache_keys": draw_cache_keys(jax.random.fold_in(key_list[12], 71), 0),
        "cache_values": noise(key_list[7], (KVH, CACHE, HD), 4.0, 24.0, ((0, 4), (1, 8))),
        "vert_blocks": draw_vert_blocks(jax.random.fold_in(key_list[12], 71), 0),
        "vert_count": draw_vert_count(jax.random.fold_in(key_list[12], 71), 0),
        "slash_offsets": draw_slash_offsets(jax.random.fold_in(key_list[12], 71), 0),
        "slash_count": draw_slash_count(jax.random.fold_in(key_list[12], 71), 0),
    }


def reference(tokens, norm_gain, w_query, w_key, w_value, w_out, cache_keys, cache_values, vert_blocks, vert_count, slash_offsets, slash_count):
    activation = tokens.astype(jnp.float32)
    normed = (activation * lax.rsqrt(lax.optimization_barrier(jnp.mean(activation * activation, axis=-1, keepdims=True)) + 1e-05) * norm_gain).astype(jnp.bfloat16)
    queries = jnp.dot(normed, w_query, preferred_element_type=jnp.float32).astype(jnp.bfloat16)
    key_rows = jnp.dot(normed, w_key, preferred_element_type=jnp.float32).astype(jnp.bfloat16)
    value_rows = jnp.dot(normed, w_value, preferred_element_type=jnp.float32).astype(jnp.bfloat16)
    group_size = QH // KVH
    score_scale = 1.0 / math.sqrt(HD)
    query_blocks = TOKENS // BLK
    head_queries = queries.reshape(TOKENS, QH, HD).transpose(1, 0, 2)
    new_keys = key_rows.reshape(TOKENS, KVH, HD).transpose(1, 0, 2).reshape(KVH, query_blocks, BLK, HD)
    new_values = value_rows.reshape(TOKENS, KVH, HD).transpose(1, 0, 2).reshape(KVH, query_blocks, BLK, HD)
    cache_key_blocks = cache_keys.reshape(KVH, CACHE // BLK, BLK, HD)
    cache_value_blocks = cache_values.reshape(KVH, CACHE // BLK, BLK, HD)
    offsets_all = jnp.arange(SMAX + 1)
    inner_row = jnp.arange(BLK)

    def one_head(head_index):
        shared_head = head_index // group_size
        query_rows = head_queries[head_index]
        live_entry = jnp.arange(NV) < vert_count[shared_head]
        picked = jnp.clip(vert_blocks[shared_head], 0, CACHE // BLK - 1)
        far_keys = jnp.take(cache_key_blocks[shared_head], picked, axis=0).reshape(NV * BLK, HD)
        far_values = jnp.take(cache_value_blocks[shared_head], picked, axis=0).reshape(NV * BLK, HD)
        far_scores = jnp.dot(query_rows, far_keys.T, preferred_element_type=jnp.float32) * score_scale
        far_scores = jnp.where(jnp.repeat(live_entry, BLK)[None, :], far_scores, -jnp.inf)
        padded_keys = jnp.concatenate([jnp.zeros((SMAX, BLK, HD), jnp.bfloat16), new_keys[shared_head]], 0)
        padded_values = jnp.concatenate([jnp.zeros((SMAX, BLK, HD), jnp.bfloat16), new_values[shared_head]], 0)
        window_keys = jnp.stack([padded_keys[SMAX - offset:SMAX - offset + query_blocks] for offset in range(SMAX + 1)], 0)
        window_values = jnp.stack([padded_values[SMAX - offset:SMAX - offset + query_blocks] for offset in range(SMAX + 1)], 0)
        blocked_queries = query_rows.reshape(query_blocks, BLK, HD).astype(jnp.float32)
        near_scores = jnp.einsum('bih,objh->bioj', blocked_queries, window_keys.astype(jnp.float32)) * score_scale
        slash_hit = jnp.any((slash_offsets[shared_head][None, :] == offsets_all[:, None]) & (jnp.arange(SMAX)[None, :] < slash_count[shared_head]), axis=1)
        exists = jnp.arange(query_blocks)[:, None] - offsets_all[None, :] >= 0
        causal = inner_row[:, None] >= inner_row[None, :]
        allowed = exists[:, None, :, None] & (slash_hit[None, None, :, None] | (offsets_all == 0)[None, None, :, None] & causal[None, :, None, :])
        near_scores = jnp.where(allowed, near_scores, -jnp.inf).reshape(TOKENS, (SMAX + 1) * BLK)
        row_max = jnp.maximum(lax.optimization_barrier(jnp.max(far_scores, axis=1)), lax.optimization_barrier(jnp.max(near_scores, axis=1)))
        far_weights = jnp.exp(far_scores - row_max[:, None])
        near_weights = jnp.exp(near_scores - row_max[:, None])
        weight_sum = lax.optimization_barrier(jnp.sum(far_weights, axis=1)) + lax.optimization_barrier(jnp.sum(near_weights, axis=1))
        mixed_out = jnp.dot(far_weights.astype(jnp.bfloat16), far_values, preferred_element_type=jnp.float32)
        near_rounded = near_weights.astype(jnp.bfloat16).astype(jnp.float32).reshape(query_blocks, BLK, SMAX + 1, BLK)
        mixed_out = mixed_out + jnp.einsum('bioj,objh->bih', near_rounded, window_values.astype(jnp.float32)).reshape(TOKENS, HD)
        return (mixed_out / weight_sum[:, None]).astype(jnp.bfloat16)
    attended = lax.map(one_head, jnp.arange(QH))
    attended = attended.transpose(1, 0, 2).reshape(TOKENS, QH * HD)
    return jnp.dot(attended, w_out, preferred_element_type=jnp.float32).astype(jnp.bfloat16)
```

```python
import functools
import math

import jax
import jax.numpy as jnp
from jax import lax
from jax.experimental import pallas as pl
from jax.experimental.pallas import tpu as pltpu
from jax.sharding import PartitionSpec as P

BLK = 64
VCAP = 8
SMAX = 4
MESH = pl.DeviceIdType.MESH


def pick_kernel(seq, vb, vc, so, sc, ck, cv, kv, table, sems):
    heads, per_device = ck.shape[0], ck.shape[1] // BLK
    first = seq[0] * per_device
    entries = vb.shape[1]
    for i in range(table.shape[0]):
        table[i] = 0
    owners = (table.shape[0] - heads * 8) // heads
    for g in range(heads):
        for r in range(VCAP):
            table[owners * heads + g * 8 + r] = 0

        def scan(e, n):
            block = vb[g, e]
            live = (e < vc[g]) & (block >= 0)
            owner = jnp.where(live, block // per_device, 0)
            spot = g * owners + owner
            table[spot] = table[spot] + live.astype(jnp.int32)
            mine = live & (block >= first) & (block < first + per_device)

            @pl.when(mine)
            def _():
                table[owners * heads + g * 8 + n] = block - first

            return n + mine.astype(jnp.int32)

        lax.fori_loop(0, entries, scan, jnp.int32(0))
        for r in range(VCAP):
            row = pl.multiple_of(table[owners * heads + g * 8 + r] * BLK, BLK)
            for j, src in enumerate((ck, cv)):
                pltpu.make_async_copy(
                    src.at[g, pl.ds(row, BLK)],
                    kv.at[g, j, pl.ds(r * BLK, BLK)],
                    sems.at[g, j, r],
                ).start()
    for g in range(heads):
        for r in range(VCAP):
            for j, src in enumerate((ck, cv)):
                pltpu.make_async_copy(
                    src.at[g, pl.ds(0, BLK)],
                    kv.at[g, j, pl.ds(r * BLK, BLK)],
                    sems.at[g, j, r],
                ).wait()
    for g in range(heads):
        for o in range(SMAX + 1):
            hit = jnp.int32(0)
            for e in range(so.shape[1]):
                hit = hit | ((so[g, e] == o) & (e < sc[g])).astype(jnp.int32)
            table[owners * heads + g * 8 + o] = hit


def layer_kernel(
    n,
    chips,
    table,
    gain,
    tok_hbm,
    wq_hbm,
    wk_hbm,
    wv_hbm,
    wo_hbm,
    kv_hbm,
    out,
    tok,
    normed,
    wq,
    wk,
    wv,
    wo,
    kv,
    near,
    prev,
    q,
    acc,
    mx,
    sm,
    att,
    core_out,
    core_in,
    x_out,
    x_in,
    part,
    load_sem,
    own_sem,
    send_sem,
    recv_sem,
    near_send,
    near_recv,
    core_send,
    core_recv,
    x_send,
    x_recv,
):
    head = lax.axis_index("heads")
    seq = lax.axis_index("seq")
    col, row = lax.rem(seq, 2), lax.div(seq, 2)
    other = 1 - col
    length = n // 2
    groups = kv.shape[1]
    rows, hd = acc.shape[1], acc.shape[2]
    qheads = acc.shape[0]
    per = qheads // groups
    core_peer = head + 1 - 2 * lax.rem(head, 2)
    span_heads = 2 * chips

    def chip_peer(h, step):
        return lax.rem(h + 2 * step, span_heads)

    tile = wq.shape[1] // 4

    loads = [
        pltpu.make_async_copy(tok_hbm, tok, load_sem.at[0]),
        pltpu.make_async_copy(wk_hbm, wk, load_sem.at[1]),
        pltpu.make_async_copy(wv_hbm, wv, load_sem.at[2]),
    ]
    for j in range(4):
        cols = pl.ds(j * tile, tile)
        loads.append(pltpu.make_async_copy(wq_hbm.at[:, cols], wq.at[:, cols], load_sem.at[3 + j]))
    loads.append(pltpu.make_async_copy(wo_hbm, wo, load_sem.at[7]))
    own = pltpu.make_async_copy(kv_hbm, kv.at[seq], own_sem)
    own.start()
    for copy in loads:
        copy.start()

    barrier = pltpu.get_barrier_semaphore()

    def greet(h, s):
        pl.semaphore_signal(barrier, inc=1, device_id=(h, s), device_id_type=MESH)

    greet(core_peer, seq)
    for step in range(1, chips):
        greet(chip_peer(head, step), seq)
    greet(head, row * 2 + other)

    @pl.when(row > 0)
    def _():
        greet(head, seq - 2)

    @pl.when(row < length - 1)
    def _():
        greet(head, seq + 2)

    @pl.when(seq > 0)
    def _():
        greet(head, seq - 1)

    @pl.when(seq < n - 1)
    def _():
        greet(head, seq + 1)

    def flag(c):
        return jnp.where(c, 1, 0)

    pl.semaphore_wait(
        barrier,
        chips + 1 + flag(row > 0) + flag(row < length - 1) + flag(seq > 0) + flag(seq < n - 1),
    )

    def hop(s, g, way):
        target = (seq + 2, seq - 2, row * 2 + other)[way]
        return pltpu.make_async_remote_copy(
            src_ref=kv.at[s, g],
            dst_ref=kv.at[s, g],
            send_sem=send_sem.at[way, s, g],
            recv_sem=recv_sem.at[s, g],
            device_id=(head, target),
            device_id_type=MESH,
        )

    own.wait()
    for g in range(groups):

        @pl.when(row < length - 1)
        def _():
            hop(seq, g, 0).start()

        @pl.when(row > 0)
        def _():
            hop(seq, g, 1).start()

        hop(seq, g, 2).start()

    loads[0].wait()

    @pl.loop(0, rows // 32)
    def _(i):
        span = pl.ds(pl.multiple_of(i * 32, 32), 32)
        a = tok[span, :].astype(jnp.float32)
        scale = lax.rsqrt(jnp.mean(a * a, axis=-1, keepdims=True) + 1e-05)
        normed[span, :] = (a * scale * gain[...]).astype(jnp.bfloat16)

    for j, w in enumerate((wk, wv)):
        loads[1 + j].wait()
        res = jnp.dot(normed[...], w[...], preferred_element_type=jnp.float32).astype(jnp.bfloat16)
        for g in range(groups):
            near[g, j] = res[:, g * hd : (g + 1) * hd]

    for j in range(4):
        loads[3 + j].wait()
        res = jnp.dot(
            normed[...], wq[:, j * tile : (j + 1) * tile], preferred_element_type=jnp.float32
        ).astype(jnp.bfloat16)
        for k in range(tile // hd):
            q[j * (tile // hd) + k] = res[:, k * hd : (k + 1) * hd]
        if j == 0:
            shift = pltpu.make_async_remote_copy(
                src_ref=near,
                dst_ref=prev,
                send_sem=near_send,
                recv_sem=near_recv,
                device_id=(head, jnp.where(seq < n - 1, seq + 1, seq - 1)),
                device_id_type=MESH,
            )

            @pl.when(seq < n - 1)
            def _():
                shift.start()

    factor = math.log2(math.e) / math.sqrt(hd)

    def fold(h, scores, values):
        old = mx[h]
        new = jnp.maximum(old, jnp.max(scores, axis=-1, keepdims=True))
        decay = jnp.exp2((old - new) * factor)
        weights = jnp.exp2((scores - new) * factor)
        sm[h] = sm[h] * decay + jnp.sum(weights, axis=-1, keepdims=True)
        acc[h] = acc[h] * decay + jnp.dot(
            weights.astype(jnp.bfloat16), values, preferred_element_type=jnp.float32
        )
        mx[h] = new

    def similar(h, keys):
        return lax.dot_general(
            q[h], keys, (((1,), (1,)), ((), ())), preferred_element_type=jnp.float32
        )

    shape = (rows, rows)
    t_index = lax.broadcasted_iota(jnp.int32, shape, 0)
    u_index = lax.broadcasted_iota(jnp.int32, shape, 1)
    gap = t_index // BLK - u_index // BLK

    def permitted(g, offset):
        hits = jnp.zeros(shape, jnp.int32)
        for o in range(SMAX + 1):
            hits = jnp.where(gap + offset == o, table[n * groups + g * 8 + o], hits)
        return hits

    for g in range(groups):
        allowed = (permitted(g, 0) > 0) | ((gap == 0) & (u_index <= t_index))

        def first(k, _):
            h = g * per + k
            scores = jnp.where(allowed, similar(h, near[g, 0]), -jnp.inf)
            new = jnp.max(scores, axis=-1, keepdims=True)
            weights = jnp.exp2((scores - new) * factor)
            mx[h] = new
            sm[h] = jnp.sum(weights, axis=-1, keepdims=True)
            acc[h] = jnp.dot(
                weights.astype(jnp.bfloat16), near[g, 1], preferred_element_type=jnp.float32
            )
            return 0

        lax.fori_loop(0, per, first, 0)

    slots = kv.shape[3]
    slot_index = lax.broadcasted_iota(jnp.int32, (1, slots), 1)

    def attend(s, g):
        live = slot_index < table[g * n + s] * BLK

        def step(k, _):
            h = g * per + k
            fold(h, jnp.where(live, similar(h, kv[s, g, 0]), -jnp.inf), kv[s, g, 1])
            return 0

        lax.fori_loop(0, per, step, 0)

    for g in range(groups):
        attend(seq, g)

    def reach(t, d):
        r = row + t if d else row - t
        return r, (r >= 0) & (r < length)

    def rounds(t, _):
        for g in range(groups):
            for d in range(2):
                r, ok = reach(t, d)

                @pl.when(ok)
                def _():
                    s = r * 2 + col
                    hop(s, g, 2).wait_recv()

                    @pl.when((row > 0) if d else (row < length - 1))
                    def _():
                        hop(s, g, 1 if d else 0).start()

                    hop(s, g, 2).start()

            for d in range(2):
                r, ok = reach(t, d)

                @pl.when(ok)
                def _():
                    attend(r * 2 + col, g)

            for d in range(2):
                r, ok = reach(t - 1, d)
                once = ok if d else ok & (t > 1)

                @pl.when(once)
                def _():
                    s = r * 2 + other
                    hop(s, g, 2).wait_recv()
                    attend(s, g)

        @pl.when(t == 1)
        def _():
            @pl.when(seq > 0)
            def _():
                shift.wait_recv()
                for g in range(groups):
                    allowed = permitted(g, rows // BLK) > 0

                    def before(k, _):
                        h = g * per + k
                        fold(h, jnp.where(allowed, similar(h, prev[g, 0]), -jnp.inf), prev[g, 1])
                        return 0

                    lax.fori_loop(0, per, before, 0)

        return 0

    lax.fori_loop(1, length + 1, rounds, 0)

    for h in range(qheads):
        att[:, h * hd : (h + 1) * hd] = (acc[h] / sm[h]).astype(jnp.bfloat16)

    loads[7].wait()
    width = part.shape[2]
    pieces = out.shape[1] // width

    def product(target, j):
        start = pl.multiple_of(target * out.shape[1] + j * width, width)
        return jnp.dot(att[...], wo[:, pl.ds(start, width)], preferred_element_type=jnp.float32)

    def core_copy(i):
        return pltpu.make_async_remote_copy(
            src_ref=core_out.at[i],
            dst_ref=core_in.at[i],
            send_sem=core_send.at[i],
            recv_sem=core_recv.at[i],
            device_id=(core_peer, seq),
            device_id_type=MESH,
        )

    def x_copy(step, j):
        i = (step - 1) * pieces + j
        return pltpu.make_async_remote_copy(
            src_ref=x_out.at[i],
            dst_ref=x_in.at[i],
            send_sem=x_send.at[i],
            recv_sem=x_recv.at[i],
            device_id=(chip_peer(head, step), seq),
            device_id_type=MESH,
        )

    todo = [(step, j) for step in range(1, chips + 1) for j in range(pieces)]

    def exchange(i):
        step, j = todo[i]
        core_out[i] = product(chip_peer(core_peer, step), j).astype(jnp.bfloat16)
        part[i] = product(chip_peer(head, step), j)
        core_copy(i).start()

    def combine(i):
        step, j = todo[i]
        core_copy(i).wait_recv()
        both = part[i] + core_in[i].astype(jnp.float32)
        if step < chips:
            x_out[i] = both.astype(jnp.bfloat16)
        else:
            part[i] = both

    for i in range(len(todo)):
        exchange(i)
        if i > 0:
            combine(i - 1)
        if i > 1 and todo[i - 2][0] < chips:
            x_copy(*todo[i - 2]).start()
    combine(len(todo) - 1)
    if pieces == 1:
        x_copy(*todo[-2]).start()
    for j in range(pieces):
        total = part[len(todo) - pieces + j]
        for step in range(1, chips):
            x_copy(step, j).wait_recv()
            total = total + x_in[(step - 1) * pieces + j].astype(jnp.float32)
        out[:, j * width : (j + 1) * width] = total.astype(jnp.bfloat16)
    for i, (step, j) in enumerate(todo):
        core_copy(i).wait_send()
        if step < chips:
            x_copy(step, j).wait_send()

    @pl.when(seq < n - 1)
    def _():
        shift.wait_send()

    def settle(t, _):
        for g in range(groups):
            for d in range(2):
                r, ok = reach(t, d)
                once = ok if d else ok & (t > 0)

                @pl.when(once)
                def _():
                    s = r * 2 + col
                    hop(s, g, 2).wait_send()

                    @pl.when((row > 0) & ((t == 0) | (d == 1)))
                    def _():
                        hop(s, g, 1).wait_send()

                    @pl.when((row < length - 1) & ((t == 0) | (d == 0)))
                    def _():
                        hop(s, g, 0).wait_send()

        return 0

    lax.fori_loop(0, length, settle, 0)


def local(
    n,
    chips,
    tokens,
    norm_gain,
    w_query,
    w_key,
    w_value,
    w_out,
    cache_keys,
    cache_values,
    vert_blocks,
    vert_count,
    slash_offsets,
    slash_count,
):
    groups, _, hd = cache_keys.shape
    rows, model = tokens.shape
    qcols = w_query.shape[1]
    qheads = qcols // hd
    out_cols = w_out.shape[1] // (2 * chips)
    slots = VCAP * BLK
    bf16, f32 = jnp.bfloat16, jnp.float32
    smem = pl.BlockSpec(memory_space=pltpu.SMEM)
    vmem = pl.BlockSpec(memory_space=pltpu.VMEM)
    hbm = pl.BlockSpec(memory_space=pl.ANY)
    seq = lax.axis_index("seq").astype(jnp.int32).reshape(1)
    kv, table = pl.pallas_call(
        pick_kernel,
        out_shape=(
            jax.ShapeDtypeStruct((groups, 2, slots, hd), bf16),
            jax.ShapeDtypeStruct((groups * n + groups * 8,), jnp.int32),
        ),
        in_specs=[smem] * 5 + [hbm] * 2,
        out_specs=(vmem, smem),
        scratch_shapes=[pltpu.SemaphoreType.DMA((groups, 2, VCAP))],
        compiler_params=pltpu.CompilerParams(vmem_limit_bytes=4 << 20),
        name="pick",
    )(seq, vert_blocks, vert_count, slash_offsets, slash_count, cache_keys, cache_values)
    pieces = 2
    width = out_cols // pieces
    dma = pltpu.SemaphoreType.DMA
    return pl.pallas_call(
        functools.partial(layer_kernel, n, chips),
        out_shape=jax.ShapeDtypeStruct((rows, out_cols), bf16),
        in_specs=[smem, vmem] + [hbm] * 6,
        out_specs=vmem,
        scratch_shapes=[
            pltpu.VMEM((rows, model), bf16),
            pltpu.VMEM((rows, model), bf16),
            pltpu.VMEM(w_query.shape, bf16),
            pltpu.VMEM(w_key.shape, bf16),
            pltpu.VMEM(w_value.shape, bf16),
            pltpu.VMEM(w_out.shape, bf16),
            pltpu.VMEM((n, groups, 2, slots, hd), bf16),
            pltpu.VMEM((groups, 2, rows, hd), bf16),
            pltpu.VMEM((groups, 2, rows, hd), bf16),
            pltpu.VMEM((qheads, rows, hd), bf16),
            pltpu.VMEM((qheads, rows, hd), f32),
            pltpu.VMEM((qheads, rows, 1), f32),
            pltpu.VMEM((qheads, rows, 1), f32),
            pltpu.VMEM((rows, qcols), bf16),
            pltpu.VMEM((chips * pieces, rows, width), bf16),
            pltpu.VMEM((chips * pieces, rows, width), bf16),
            pltpu.VMEM(((chips - 1) * pieces, rows, width), bf16),
            pltpu.VMEM(((chips - 1) * pieces, rows, width), bf16),
            pltpu.VMEM((chips * pieces, rows, width), f32),
            dma((8,)),
            dma(()),
            dma((3, n, groups)),
            dma((n, groups)),
            dma(()),
            dma(()),
            dma((chips * pieces,)),
            dma((chips * pieces,)),
            dma(((chips - 1) * pieces,)),
            dma(((chips - 1) * pieces,)),
        ],
        compiler_params=pltpu.CompilerParams(
            collective_id=0, has_side_effects=True, vmem_limit_bytes=60 << 20
        ),
        name="layer",
    )(table, norm_gain.reshape(1, model), tokens, w_query, w_key, w_value, w_out, kv)


def solution(mesh):
    return jax.shard_map(
        functools.partial(local, mesh.shape["seq"], mesh.shape["heads"] // 2),
        mesh=mesh,
        in_specs=(
            P("seq", None),
            P(),
            P(None, "heads"),
            P(None, "heads"),
            P(None, "heads"),
            P("heads", None),
            P("heads", "seq", None),
            P("heads", "seq", None),
            P("heads", None),
            P("heads"),
            P("heads", None),
            P("heads"),
        ),
        out_specs=P("seq", "heads"),
        check_vma=False,
    )
```

```python
import functools
import math

import jax
import jax.numpy as jnp
from jax import lax
from jax.experimental import pallas as pl
from jax.experimental.pallas import tpu as pltpu
from jax.sharding import PartitionSpec as P

BLK = 64
VCAP = 8
SMAX = 4
MESH = pl.DeviceIdType.MESH


def pick_kernel(seq, vb, vc, so, sc, ck, cv, kv, table, sems):
    heads, per_device = ck.shape[0], ck.shape[1] // BLK
    first = seq[0] * per_device
    entries = vb.shape[1]
    for i in range(table.shape[0]):
        table[i] = 0
    owners = (table.shape[0] - heads * 8) // heads
    for g in range(heads):
        for r in range(VCAP):
            table[owners * heads + g * 8 + r] = 0

        def scan(e, n):
            block = vb[g, e]
            live = (e < vc[g]) & (block >= 0)
            owner = jnp.where(live, block // per_device, 0)
            spot = g * owners + owner
            table[spot] = table[spot] + live.astype(jnp.int32)
            mine = live & (block >= first) & (block < first + per_device)

            @pl.when(mine)
            def _():
                table[owners * heads + g * 8 + n] = block - first

            return n + mine.astype(jnp.int32)

        lax.fori_loop(0, entries, scan, jnp.int32(0))
        for r in range(VCAP):
            row = pl.multiple_of(table[owners * heads + g * 8 + r] * BLK, BLK)
            for j, src in enumerate((ck, cv)):
                pltpu.make_async_copy(
                    src.at[g, pl.ds(row, BLK)],
                    kv.at[g, j, pl.ds(r * BLK, BLK)],
                    sems.at[g, j, r],
                ).start()
    for g in range(heads):
        for r in range(VCAP):
            for j, src in enumerate((ck, cv)):
                pltpu.make_async_copy(
                    src.at[g, pl.ds(0, BLK)],
                    kv.at[g, j, pl.ds(r * BLK, BLK)],
                    sems.at[g, j, r],
                ).wait()
    for g in range(heads):
        for o in range(SMAX + 1):
            hit = jnp.int32(0)
            for e in range(so.shape[1]):
                hit = hit | ((so[g, e] == o) & (e < sc[g])).astype(jnp.int32)
            table[owners * heads + g * 8 + o] = hit


def layer_kernel(
    n,
    chips,
    table,
    gain,
    tok_hbm,
    wq_hbm,
    wk_hbm,
    wv_hbm,
    wo_hbm,
    kv_hbm,
    out,
    tok,
    normed,
    wq,
    wk,
    wv,
    wo,
    kv,
    near,
    prev,
    q,
    acc,
    mx,
    sm,
    att,
    core_out,
    core_in,
    x_out,
    x_in,
    part,
    load_sem,
    own_sem,
    send_sem,
    recv_sem,
    near_send,
    near_recv,
    core_send,
    core_recv,
    x_send,
    x_recv,
):
    head = lax.axis_index("heads")
    seq = lax.axis_index("seq")
    col, row = lax.rem(seq, 2), lax.div(seq, 2)
    other = 1 - col
    length = n // 2
    groups = kv.shape[1]
    hd, rows = acc.shape[1], acc.shape[2]
    qheads = acc.shape[0]
    per = qheads // groups
    mate = row + 1 - 2 * lax.rem(row, 2)
    up = mate > row
    core_peer = head + 1 - 2 * lax.rem(head, 2)
    span_heads = 2 * chips

    def chip_peer(h, step):
        return lax.rem(h + 2 * step, span_heads)

    tile = wq.shape[1] // 4

    loads = [
        pltpu.make_async_copy(tok_hbm, tok, load_sem.at[0]),
        pltpu.make_async_copy(wk_hbm, wk, load_sem.at[1]),
        pltpu.make_async_copy(wv_hbm, wv, load_sem.at[2]),
    ]
    for j in range(4):
        cols = pl.ds(j * tile, tile)
        loads.append(pltpu.make_async_copy(wq_hbm.at[:, cols], wq.at[:, cols], load_sem.at[3 + j]))
    loads.append(pltpu.make_async_copy(wo_hbm, wo, load_sem.at[7]))
    own = pltpu.make_async_copy(kv_hbm, kv.at[seq], own_sem)
    own.start()
    for copy in loads[:4]:
        copy.start()

    barrier = pltpu.get_barrier_semaphore()

    def greet(h, s):
        pl.semaphore_signal(barrier, inc=1, device_id=(h, s), device_id_type=MESH)

    greet(core_peer, seq)
    for step in range(1, chips):
        greet(chip_peer(head, step), seq)
    greet(head, row * 2 + other)

    @pl.when(row > 0)
    def _():
        greet(head, seq - 2)

    @pl.when(row < length - 1)
    def _():
        greet(head, seq + 2)

    @pl.when(seq > 0)
    def _():
        greet(head, seq - 1)

    @pl.when(seq < n - 1)
    def _():
        greet(head, seq + 1)

    def flag(c):
        return jnp.where(c, 1, 0)

    pl.semaphore_wait(
        barrier,
        chips + 1 + flag(row > 0) + flag(row < length - 1) + flag(seq > 0) + flag(seq < n - 1),
    )

    def hop(s, g, way):
        target = (seq + 2, seq - 2, row * 2 + other)[way]
        return pltpu.make_async_remote_copy(
            src_ref=kv.at[s, g],
            dst_ref=kv.at[s, g],
            send_sem=send_sem.at[way, s, g],
            recv_sem=recv_sem.at[s, g],
            device_id=(head, target),
            device_id_type=MESH,
        )

    own.wait()
    for g in range(groups):

        @pl.when(row < length - 1)
        def _():
            hop(seq, g, 0).start()

        @pl.when(row > 0)
        def _():
            hop(seq, g, 1).start()

        hop(seq, g, 2).start()

    loads[0].wait()
    for copy in loads[4:]:
        copy.start()

    @pl.loop(0, rows // 32)
    def _(i):
        span = pl.ds(pl.multiple_of(i * 32, 32), 32)
        a = tok[span, :].astype(jnp.float32)
        scale = lax.rsqrt(jnp.mean(a * a, axis=-1, keepdims=True) + 1e-05)
        normed[span, :] = (a * scale * gain[...]).astype(jnp.bfloat16)

    for j, w in enumerate((wk, wv)):
        loads[1 + j].wait()
        res = jnp.dot(normed[...], w[...], preferred_element_type=jnp.float32).astype(jnp.bfloat16)
        for g in range(groups):
            near[g, j] = res[:, g * hd : (g + 1) * hd]

    for j in range(4):
        loads[3 + j].wait()
        res = jnp.dot(
            normed[...], wq[:, j * tile : (j + 1) * tile], preferred_element_type=jnp.float32
        ).astype(jnp.bfloat16)
        for k in range(tile // hd):
            q[j * (tile // hd) + k] = res[:, k * hd : (k + 1) * hd]
        if j == 0:
            shift = pltpu.make_async_remote_copy(
                src_ref=near,
                dst_ref=prev,
                send_sem=near_send,
                recv_sem=near_recv,
                device_id=(head, jnp.where(seq < n - 1, seq + 1, seq - 1)),
                device_id_type=MESH,
            )

            @pl.when(seq < n - 1)
            def _():
                shift.start()

    def reach(t, d):
        r = row + t * (2 * d - 1)
        return r, (r >= 0) & (r < length)

    def across(r, g):
        return (r != mate) | (g < groups - 1)

    def relay(t):
        for g in range(groups):
            for d in range(2):
                r, ok = reach(t, d)

                @pl.when(ok)
                def _():
                    s = r * 2 + col
                    hop(s, g, 2).wait_recv()

                    @pl.when((row > 0) if d else (row < length - 1))
                    def _():
                        hop(s, g, 1 if d else 0).start()

                    @pl.when(across(r, g))
                    def _():
                        hop(s, g, 2).start()

    relay(1)

    factor = math.log2(math.e) / math.sqrt(hd)

    def fold(g, keys, values, allowed):
        heads = [g * per + k for k in range(per)]
        old = [(mx[h], sm[h], acc[h]) for h in heads]
        fresh = []
        for h, (m, l, a) in zip(heads, old):
            scores = lax.dot_general(
                keys, q[h], (((1,), (1,)), ((), ())), preferred_element_type=jnp.float32
            )
            scores = jnp.where(allowed, scores, -jnp.inf)
            new = jnp.maximum(m, jnp.max(scores, axis=0, keepdims=True))
            decay = jnp.exp2((m - new) * factor)
            weights = jnp.exp2((scores - new) * factor)
            l = l * decay + jnp.sum(weights, axis=0, keepdims=True)
            a = a * decay + lax.dot_general(
                values,
                weights.astype(jnp.bfloat16),
                (((0,), (0,)), ((), ())),
                preferred_element_type=jnp.float32,
            )
            fresh.append((new, l, a))
        for h, (m, l, a) in zip(heads, fresh):
            mx[h], sm[h], acc[h] = m, l, a

    shape = (rows, rows)
    u_index = lax.broadcasted_iota(jnp.int32, shape, 0)
    t_index = lax.broadcasted_iota(jnp.int32, shape, 1)
    gap = t_index // BLK - u_index // BLK
    mx[...] = jnp.full(mx.shape, -1e30, jnp.float32)
    sm[...] = jnp.zeros(sm.shape, jnp.float32)
    acc[...] = jnp.zeros(acc.shape, jnp.float32)

    def spans(g, rows_ref, offset):
        hits = jnp.zeros(shape, jnp.int32)
        for o in range(SMAX + 1):
            hits = jnp.where(gap + offset == o, table[n * groups + g * 8 + o], hits)
        causal = (gap + offset == 0) & (u_index <= t_index)
        fold(g, rows_ref[g, 0], rows_ref[g, 1], (hits > 0) | causal)
        return 0

    lax.fori_loop(0, groups, lambda g, _: spans(g, near, 0), 0)

    slots = kv.shape[3]
    slot_index = lax.broadcasted_iota(jnp.int32, (slots, rows), 0)

    def attend(s, g):
        fold(g, kv[s, g, 0], kv[s, g, 1], slot_index < table[g * n + s] * BLK)

    def own_shard(g, _):
        attend(seq, g)
        return 0

    lax.fori_loop(0, groups, own_shard, 0)

    def visit(t, side, wait):
        def one(i, _):
            g, d = lax.div(i, 2), lax.rem(i, 2)
            r, ok = reach(t, d)
            if wait:
                ok = ok & ((t > 0) | (d == 0)) & across(r, g)

            @pl.when(ok)
            def _():
                s = r * 2 + side
                if wait:
                    hop(s, g, 2).wait_recv()
                attend(s, g)

            return 0

        lax.fori_loop(0, 2 * groups, one, 0)

    def rounds(t, _):
        visit(t, col, False)

        @pl.when(t < length - 1)
        def _():
            relay(t + 1)

        visit(t - 1, other, True)

        @pl.when((t == 1) & (seq > 0))
        def _():
            shift.wait_recv()
            lax.fori_loop(0, groups, lambda g, _: spans(g, prev, rows // BLK), 0)

        @pl.when((t == max(length - 2, 1)) & up)
        def _():
            hop(row * 2 + other, groups - 1, 0).start()

        @pl.when((t == max(length - 2, 1)) & jnp.logical_not(up))
        def _():
            hop(row * 2 + other, groups - 1, 1).start()

        return 0

    lax.fori_loop(1, length + 1, rounds, 0)
    last = mate * 2 + other
    hop(last, groups - 1, 2).wait_recv()
    attend(last, groups - 1)

    for h in range(qheads):
        att[:, h * hd : (h + 1) * hd] = jnp.transpose(acc[h] / sm[h]).astype(jnp.bfloat16)

    loads[7].wait()
    width = part.shape[2]
    pieces = out.shape[1] // width

    def product(target, j):
        start = pl.multiple_of(target * out.shape[1] + j * width, width)
        return jnp.dot(att[...], wo[:, pl.ds(start, width)], preferred_element_type=jnp.float32)

    def core_copy(i):
        return pltpu.make_async_remote_copy(
            src_ref=core_out.at[i],
            dst_ref=core_in.at[i],
            send_sem=core_send.at[i],
            recv_sem=core_recv.at[i],
            device_id=(core_peer, seq),
            device_id_type=MESH,
        )

    def x_copy(step, j):
        i = (step - 1) * pieces + j
        return pltpu.make_async_remote_copy(
            src_ref=x_out.at[i],
            dst_ref=x_in.at[i],
            send_sem=x_send.at[i],
            recv_sem=x_recv.at[i],
            device_id=(chip_peer(head, step), seq),
            device_id_type=MESH,
        )

    todo = [(step, j) for step in range(1, chips + 1) for j in range(pieces)]

    def exchange(i):
        step, j = todo[i]
        core_out[i] = product(chip_peer(core_peer, step), j).astype(jnp.bfloat16)
        part[i] = product(chip_peer(head, step), j)
        core_copy(i).start()

    def combine(i):
        step, j = todo[i]
        core_copy(i).wait_recv()
        both = part[i] + core_in[i].astype(jnp.float32)
        if step < chips:
            x_out[i] = both.astype(jnp.bfloat16)
        else:
            part[i] = both

    for i in range(len(todo)):
        exchange(i)
        if i > 0:
            combine(i - 1)
        if i > 1 and todo[i - 2][0] < chips:
            x_copy(*todo[i - 2]).start()
    combine(len(todo) - 1)
    if pieces == 1:
        x_copy(*todo[-2]).start()
    for j in range(pieces):
        total = part[len(todo) - pieces + j]
        for step in range(1, chips):
            x_copy(step, j).wait_recv()
            total = total + x_in[(step - 1) * pieces + j].astype(jnp.float32)
        out[:, j * width : (j + 1) * width] = total.astype(jnp.bfloat16)
    for i, (step, j) in enumerate(todo):
        core_copy(i).wait_send()
        if step < chips:
            x_copy(step, j).wait_send()

    @pl.when(seq < n - 1)
    def _():
        shift.wait_send()

    def settle(t, _):
        for g in range(groups):
            for d in range(2):
                r, ok = reach(t, d)
                once = ok if d else ok & (t > 0)

                @pl.when(once)
                def _():
                    s = r * 2 + col

                    @pl.when(across(r, g))
                    def _():
                        hop(s, g, 2).wait_send()

                    @pl.when((row > 0) & ((t == 0) | (d == 1)))
                    def _():
                        hop(s, g, 1).wait_send()

                    @pl.when((row < length - 1) & ((t == 0) | (d == 0)))
                    def _():
                        hop(s, g, 0).wait_send()

        return 0

    lax.fori_loop(0, length, settle, 0)

    @pl.when(up)
    def _():
        hop(row * 2 + other, groups - 1, 0).wait_send()

    @pl.when(jnp.logical_not(up))
    def _():
        hop(row * 2 + other, groups - 1, 1).wait_send()


def local(
    n,
    chips,
    tokens,
    norm_gain,
    w_query,
    w_key,
    w_value,
    w_out,
    cache_keys,
    cache_values,
    vert_blocks,
    vert_count,
    slash_offsets,
    slash_count,
):
    groups, _, hd = cache_keys.shape
    rows, model = tokens.shape
    qcols = w_query.shape[1]
    qheads = qcols // hd
    out_cols = w_out.shape[1] // (2 * chips)
    slots = VCAP * BLK
    bf16, f32 = jnp.bfloat16, jnp.float32
    smem = pl.BlockSpec(memory_space=pltpu.SMEM)
    vmem = pl.BlockSpec(memory_space=pltpu.VMEM)
    hbm = pl.BlockSpec(memory_space=pl.ANY)
    seq = lax.axis_index("seq").astype(jnp.int32).reshape(1)
    kv, table = pl.pallas_call(
        pick_kernel,
        out_shape=(
            jax.ShapeDtypeStruct((groups, 2, slots, hd), bf16),
            jax.ShapeDtypeStruct((groups * n + groups * 8,), jnp.int32),
        ),
        in_specs=[smem] * 5 + [hbm] * 2,
        out_specs=(vmem, smem),
        scratch_shapes=[pltpu.SemaphoreType.DMA((groups, 2, VCAP))],
        compiler_params=pltpu.CompilerParams(vmem_limit_bytes=60 << 20),
        name="pick",
    )(seq, vert_blocks, vert_count, slash_offsets, slash_count, cache_keys, cache_values)
    pieces = 2
    width = out_cols // pieces
    dma = pltpu.SemaphoreType.DMA
    return pl.pallas_call(
        functools.partial(layer_kernel, n, chips),
        out_shape=jax.ShapeDtypeStruct((rows, out_cols), bf16),
        in_specs=[smem, vmem] + [hbm] * 6,
        out_specs=vmem,
        scratch_shapes=[
            pltpu.VMEM((rows, model), bf16),
            pltpu.VMEM((rows, model), bf16),
            pltpu.VMEM(w_query.shape, bf16),
            pltpu.VMEM(w_key.shape, bf16),
            pltpu.VMEM(w_value.shape, bf16),
            pltpu.VMEM(w_out.shape, bf16),
            pltpu.VMEM((n, groups, 2, slots, hd), bf16),
            pltpu.VMEM((groups, 2, rows, hd), bf16),
            pltpu.VMEM((groups, 2, rows, hd), bf16),
            pltpu.VMEM((qheads, rows, hd), bf16),
            pltpu.VMEM((qheads, hd, rows), f32),
            pltpu.VMEM((qheads, 1, rows), f32),
            pltpu.VMEM((qheads, 1, rows), f32),
            pltpu.VMEM((rows, qcols), bf16),
            pltpu.VMEM((chips * pieces, rows, width), bf16),
            pltpu.VMEM((chips * pieces, rows, width), bf16),
            pltpu.VMEM(((chips - 1) * pieces, rows, width), bf16),
            pltpu.VMEM(((chips - 1) * pieces, rows, width), bf16),
            pltpu.VMEM((chips * pieces, rows, width), f32),
            dma((8,)),
            dma(()),
            dma((3, n, groups)),
            dma((n, groups)),
            dma(()),
            dma(()),
            dma((chips * pieces,)),
            dma((chips * pieces,)),
            dma(((chips - 1) * pieces,)),
            dma(((chips - 1) * pieces,)),
        ],
        compiler_params=pltpu.CompilerParams(
            collective_id=0, has_side_effects=True, vmem_limit_bytes=60 << 20
        ),
        name="layer",
    )(table, norm_gain.reshape(1, model), tokens, w_query, w_key, w_value, w_out, kv)


def solution(mesh):
    return jax.shard_map(
        functools.partial(local, mesh.shape["seq"], mesh.shape["heads"] // 2),
        mesh=mesh,
        in_specs=(
            P("seq", None),
            P(),
            P(None, "heads"),
            P(None, "heads"),
            P(None, "heads"),
            P("heads", None),
            P("heads", "seq", None),
            P("heads", "seq", None),
            P("heads", None),
            P("heads"),
            P("heads", None),
            P("heads"),
        ),
        out_specs=P("seq", "heads"),
        check_vma=False,
    )
```
